256 devices in a mesh: slab: 4 (over y_hi, core), row: 8 (over x, y_lo), col: 8 (over z).
Axes of the slice: x: 4, y: 4 (y_hi: 2, y_lo: 2; y = y_hi * 2 + y_lo), z: 8, core: 2. Of those that a mesh axis runs over, the one named last changes fastest.
Arguments:
- reflection: bfloat16 [4, 4096, 4096], P('slab', 'row', 'col'), may hold values from -0.0625 to 0.0625
- transmission: bfloat16 [4, 4096, 4096], P('slab', 'row', 'col'), may hold values from -0.09375 to 0.09375
- shots: bfloat16 [4, 4096, 2048], P('slab', 'row', 'col'), may hold values from -6 to 6
Outputs:
- merged: bfloat16 [4, 4096, 2048], P('slab', 'row', 'col')
The draws below stay inside these ranges and needn't reach their ends.
All inputs are finite; a program needn't handle non-finite values.
Results may differ from the reference program's by a relative error of at most 0.008.
Values may be sent and summed in bfloat16 or wider, within the bound.
No kernel may reach another device: no remote copies, remote signals or barrier semaphores. Data moves between devices by JAX's collectives and lax.ppermute only.
A program may use at most 64 MiB of HBM per device.

```python
import jax
import jax.numpy as jnp
from jax import lax

M = 4096
SHOTS = 2048
N_SLAB = 4


def block_scale(rng, dims, split, least, largest):
    level = 1.0
    for axis_at, shards_of in split:
        draws = jax.random.uniform(jax.random.fold_in(jax.random.fold_in(rng, 6), axis_at), (shards_of,), jnp.float32, least / len(split), largest / len(split))
        level = level * jnp.repeat(jnp.exp(draws), dims[axis_at] // shards_of).reshape((-1,) + (1,) * (len(dims) - 1 - axis_at))
    return level


def bell_draw(stream_key, extent, spread, limit, split=(), held_as=jnp.bfloat16):
    entries = jax.random.normal(stream_key, extent, jnp.float32) * spread
    if len(split) > 0:
        entries = block_scale(stream_key, extent, split, -0.22, 0.18) * entries
    return jnp.clip(entries, min=-limit, max=limit).astype(held_as)


def setup_inputs(seed: int = 0) -> dict:
    seeds = jax.random.split(jax.random.key(seed), 4)
    reflection = bell_draw(seeds[0], (N_SLAB, M, M), (2 * M) ** -0.5, 0.0625, ((0, 4), (1, 8), (2, 8)))
    transmission = bell_draw(seeds[1], (N_SLAB, M, M), M ** -0.5, 0.09375, ((0, 4), (1, 8), (2, 8)))
    shots = bell_draw(seeds[2], (N_SLAB, M, SHOTS), 1.0, 6.0, ((0, 4), (1, 8), (2, 8)))
    return dict(reflection=reflection, transmission=transmission, shots=shots)


def reference(reflection, transmission, shots):
    results = []
    for slab_index in range(N_SLAB):
        partner = slab_index ^ 1
        first = jnp.dot(transmission[slab_index], shots[slab_index], preferred_element_type=jnp.float32).astype(jnp.bfloat16)
        middle = jnp.dot(reflection[partner].astype(jnp.float32), first.astype(jnp.float32), precision=lax.Precision.HIGHEST)
        bounce = jnp.dot(reflection[slab_index].astype(jnp.float32), middle, precision=lax.Precision.HIGHEST)
        summed = (first.astype(jnp.float32) + bounce).astype(jnp.bfloat16)
        results.append(jnp.dot(transmission[partner], summed, preferred_element_type=jnp.float32).astype(jnp.bfloat16))
    return jnp.stack(results)
```

```python
import functools

import jax
import jax.numpy as jnp
from jax import lax
from jax.experimental import pallas as pl
from jax.experimental.pallas import tpu as pltpu
from jax.sharding import PartitionSpec as P

BF16 = jnp.bfloat16
F32 = jnp.float32


def after(array, *deps):
    return lax.optimization_barrier((array, *deps))[0]


def z_send(block, step):
    return lax.ppermute(block, "col", [(z, (z + step) % 8) for z in range(8)])


def x_send(block, step):
    route = [(x * 2 + y, (x + step) % 4 * 2 + y) for x in range(4) for y in range(2)]
    return lax.ppermute(block, "row", route)


def y_send(block):
    return lax.ppermute(block, "row", [(r, r ^ 1) for r in range(8)])


def core_send(block):
    return lax.ppermute(block, "slab", [(s, s ^ 1) for s in range(4)])


def row_steps(tile):
    half = tile.shape[0] // 2
    side = y_send(tile)
    below = x_send(tile, -1)
    above = x_send(tile, 1)
    yield side, below, above
    above_side = x_send(side, 1)
    across = x_send(below, -1)
    below_side = y_send(below)
    yield above_side, across, below_side
    top = x_send(above_side[:half], 1)
    low = y_send(across[half:])
    yield top, low
    yield [
        (0, 0, tile),
        (1, 0, side),
        (2, 0, below),
        (6, 0, above),
        (7, 0, above_side),
        (4, 0, across),
        (3, 0, below_side),
        (5, 0, top),
        (5, half, low),
    ]


def col_steps(tile):
    half = tile.shape[0] // 2
    have = {0: tile}
    up = down = tile
    gate = ()
    for step in range(1, 4):
        if gate:
            up, down = after(up, *gate), after(down, *gate)
        down = z_send(down, -1)
        up = z_send(up, 1)
        have[step] = down
        have[8 - step] = up
        gate = yield down, up
    if gate:
        up, down = after(up, *gate), after(down, *gate)
    last = z_send(down[:half], -1), z_send(up[half:], 1)
    have[4] = jnp.concatenate(last, axis=0)
    yield last
    yield [have[step] for step in range(8)]


def gather_row(tile):
    return list(row_steps(tile))[-1]


def gather_both(col_tile, row_tile):
    col, row = col_steps(col_tile), row_steps(row_tile)
    next(col)
    for _ in range(3):
        phase = next(row)
        last = col.send(phase)
    return next(col), next(row)


def fold(pieces, added, order, operator, *refs):
    *shots, out = refs
    height = 128

    @pl.loop(0, out.shape[0] // height)
    def _(chunk):
        rows = pl.ds(pl.multiple_of(chunk * height, height), height)
        total = None
        for (place, start), shot in zip(pieces, shots):
            size = shot.shape[0]
            panel = operator[order[place], rows, start : start + size]
            term = jnp.dot(panel, shot[...], preferred_element_type=F32)
            total = term if total is None else total + term
        if added:
            total = total + shots[-1][rows, :].astype(F32)
        out[rows, :] = total.astype(out.dtype)


def multiply(operator, pieces, order, added=None):
    count, rows, depth = operator.shape
    columns = pieces[0][2].shape[1]
    shots = [piece[2] for piece in pieces] + ([] if added is None else [added])
    where = [piece[:2] for piece in pieces]
    in_vmem = pl.BlockSpec(memory_space=pltpu.VMEM)
    return pl.pallas_call(
        functools.partial(fold, where, added is not None),
        in_specs=[pl.BlockSpec(memory_space=pltpu.SMEM)] + [in_vmem] * (1 + len(shots)),
        out_specs=in_vmem,
        out_shape=jax.ShapeDtypeStruct((rows, columns), BF16),
        compiler_params=pltpu.CompilerParams(vmem_limit_bytes=24 << 20),
        cost_estimate=pl.CostEstimate(
            flops=2 * count * rows * depth * columns,
            bytes_accessed=2 * count * depth * (rows + columns),
            transcendentals=0,
        ),
    )(order, operator, *shots)


def on_device(reflection, transmission, shots):
    own_refl = reflection[0]
    own_trans = transmission[0]
    shot_tile = shots[0]
    row = lax.axis_index("row")
    x, y, z = row // 2, row % 2, lax.axis_index("col")
    place = jnp.arange(8, dtype=jnp.int32)
    block = (x + place // 2) % 4 * 2 + (y ^ place % 2)
    by_step = (block - z) % 8
    far_refl = core_send(own_refl)
    trans, incoming = gather_both(own_trans, shot_tile)
    trans = jnp.stack(trans)
    first = multiply(trans, incoming, by_step)
    far_trans = core_send(trans)
    refl, passed = gather_both(after(far_refl, trans), first)
    refl = jnp.stack(refl)
    middle = multiply(refl, passed, by_step)
    near_refl = core_send(refl)
    summed = multiply(near_refl, gather_row(middle), by_step, first)
    return multiply(far_trans, gather_row(summed), by_step)[None]


def solution(mesh):
    placed = (P("slab", "row", "col"), P("slab", "row", "col"), P("slab", "row", "col"))
    return jax.shard_map(
        on_device, mesh=mesh, in_specs=placed, out_specs=P("slab", "row", "col"), check_vma=False
    )
```

```python
import functools

import jax
import jax.numpy as jnp
from jax import lax
from jax.experimental import pallas as pl
from jax.experimental.pallas import tpu as pltpu
from jax.sharding import PartitionSpec as P

BF16 = jnp.bfloat16
F32 = jnp.float32


def after(array, *deps):
    return lax.optimization_barrier((array, *deps))[0]


def wait_all(arrays, gate):
    return [after(array, *gate) if gate else array for array in arrays]


def z_send(block, step):
    return lax.ppermute(block, "col", [(z, (z + step) % 8) for z in range(8)])


def send(block, step, side, other):
    route = []
    for slab in range(4):
        for row in range(8):
            x, y = row // 2, row % 2
            there = (x + step) % 4 * 2 + (y ^ side)
            route.append((slab * 8 + row, (slab ^ other) * 8 + there))
    return lax.ppermute(block, ("slab", "row"), route)


def core_send(block):
    return send(block, 0, 0, 1)


def row_steps(tile, other=0):
    half = tile.shape[0] // 2
    here = core_send(tile) if other else tile
    side = send(tile, 0, 1, other)
    below = send(tile, -1, 0, other)
    above = send(tile, 1, 0, other)
    gate = yield side, below, above
    side_on, below_on = wait_all((side, below), gate)
    above_side = send(side_on, 1, 0, 0)
    across = send(below_on, -1, 0, 0)
    below_side = send(below_on, 0, 1, 0)
    gate = yield above_side, across, below_side
    above_side_on, across_on = wait_all((above_side, across), gate)
    top = send(above_side_on[:half], 1, 0, 0)
    low = send(across_on[half:], 0, 1, 0)
    yield top, low
    yield [
        (0, 0, here),
        (1, 0, side),
        (2, 0, below),
        (6, 0, above),
        (7, 0, above_side),
        (4, 0, across),
        (3, 0, below_side),
        (5, 0, top),
        (5, half, low),
    ]


def col_steps(tile):
    half = tile.shape[0] // 2
    have = {0: tile}
    up = down = tile
    for step in range(1, 4):
        down = z_send(down, -1)
        up = z_send(up, 1)
        have[step] = down
        have[8 - step] = up
        gate = yield down, up
        up, down = wait_all((up, down), gate)
    top, low = z_send(down[:half], -1), z_send(up[half:], 1)
    yield [have[0], have[1], have[2], have[3], top, low, have[5], have[6], have[7]]


def gather_row(tile, other=0):
    return list(row_steps(tile, other))[-1]


def pair_steps(tile, split):
    side = send(tile, 0, 1, 0)
    gate = yield (side,)
    (pair,) = wait_all([jnp.stack([tile, side])], gate)
    below = send(pair, -1, 0, 0)
    above = send(pair, 1, 0, 0)
    gate = yield below, above
    below_on, above_on = wait_all((below, above), gate)
    if split:
        across = jnp.stack([send(below_on[0], -1, 0, 0), send(above_on[1], 1, 0, 0)])
    else:
        across = send(below_on, -1, 0, 0)
    yield (across,)
    yield jnp.concatenate([pair, below, across, above], axis=0)


def fold_tiles(order, shots, *refs):
    *tiles, out, panel, sems = refs
    half = tiles[4].shape[0]
    copies = []
    for index, tile in enumerate(tiles):
        if index in (4, 5):
            to = panel.at[4, pl.ds((index - 4) * half, half)]
        else:
            to = panel.at[index if index < 4 else index - 1]
        copies.append(pltpu.make_async_copy(tile, to, sems.at[index]))
        copies[-1].start()
    height = 128
    for side in range(2):

        @pl.loop(0, half // height)
        def _(chunk):
            start = pl.multiple_of(chunk * height, height)
            whole = pl.ds(pl.multiple_of(side * half + start, height), height)
            total = None
            for step in range(8):
                if step == 4:
                    rows = tiles[4 + side][pl.ds(start, height), :]
                else:
                    rows = tiles[step if step < 4 else step + 1][whole, :]
                term = jnp.dot(rows, shots[order[step]], preferred_element_type=F32)
                total = term if total is None else total + term
            out[whole, :] = total.astype(out.dtype)

    for copy in copies:
        copy.wait()


def multiply_tiles(tiles, shots, order):
    rows, depth = tiles[0].shape
    count, _, columns = shots.shape
    in_vmem = pl.BlockSpec(memory_space=pltpu.VMEM)
    return pl.pallas_call(
        fold_tiles,
        in_specs=[pl.BlockSpec(memory_space=pltpu.SMEM)] + [in_vmem] * (1 + len(tiles)),
        out_specs=[in_vmem, pl.BlockSpec(memory_space=pl.ANY)],
        out_shape=[
            jax.ShapeDtypeStruct((rows, columns), BF16),
            jax.ShapeDtypeStruct((count, rows, depth), BF16),
        ],
        scratch_shapes=[pltpu.SemaphoreType.DMA((len(tiles),))],
        compiler_params=pltpu.CompilerParams(vmem_limit_bytes=24 << 20),
        cost_estimate=pl.CostEstimate(
            flops=2 * count * rows * depth * columns,
            bytes_accessed=2 * count * depth * (rows + columns),
            transcendentals=0,
        ),
    )(order, shots, *tiles)


def fold(pieces, added, order, operator, *refs):
    *shots, out = refs
    height = 128

    @pl.loop(0, out.shape[-2] // height)
    def _(chunk):
        rows = pl.ds(pl.multiple_of(chunk * height, height), height)
        total = None
        for (place, start), shot in zip(pieces, shots):
            size = shot.shape[0]
            panel = operator[order[place], rows, start : start + size]
            term = jnp.dot(panel, shot[...], preferred_element_type=F32)
            total = term if total is None else total + term
        if added:
            total = total + shots[-1][rows, :].astype(F32)
        out[rows, :] = total.astype(out.dtype)


def multiply(operator, pieces, order, added=None):
    count, rows, depth = operator.shape
    columns = pieces[0][2].shape[1]
    shots = [piece[2] for piece in pieces] + ([] if added is None else [added])
    where = [piece[:2] for piece in pieces]
    in_vmem = pl.BlockSpec(memory_space=pltpu.VMEM)
    return pl.pallas_call(
        functools.partial(fold, where, added is not None),
        in_specs=[pl.BlockSpec(memory_space=pltpu.SMEM)] + [in_vmem] * (1 + len(shots)),
        out_specs=in_vmem,
        out_shape=jax.ShapeDtypeStruct((rows, columns), BF16),
        compiler_params=pltpu.CompilerParams(vmem_limit_bytes=24 << 20),
        cost_estimate=pl.CostEstimate(
            flops=2 * count * rows * depth * columns,
            bytes_accessed=2 * count * depth * (rows + columns),
            transcendentals=0,
        ),
    )(order, operator, *shots)


def on_device(reflection, transmission, shots):
    own_refl = reflection[0]
    own_trans = transmission[0]
    shot_tile = shots[0]
    row = lax.axis_index("row")
    x, y, z = row // 2, row % 2, lax.axis_index("col")
    place = jnp.arange(8, dtype=jnp.int32)
    block = (x + place // 2) % 4 * 2 + (y ^ place % 2)
    by_step = (block - z) % 8
    step_block = (place + z) % 8
    step_place = (step_block // 2 - x) % 4 * 2 + (step_block % 2 ^ y)
    far_refl = core_send(own_refl)
    ring, shot_ring = col_steps(own_trans), pair_steps(shot_tile, False)
    next(ring)
    ring.send((*next(shot_ring), far_refl))
    step = ring.send(next(shot_ring))
    trans = ring.send(next(shot_ring))
    incoming = next(shot_ring)
    ring = col_steps(after(far_refl, *step))
    step = next(ring)
    first, trans = multiply_tiles(trans, after(incoming, *step), step_place)
    first_ring = pair_steps(first, True)
    step, phase = ring.send(()), next(first_ring)
    step, phase = ring.send(phase), first_ring.send(step)
    far_first = core_send(after(first, *step))
    refl, phase = ring.send((*phase, far_first)), first_ring.send(step)
    passed = next(first_ring)
    middle, refl = multiply_tiles(refl, passed, step_place)
    summed = multiply(refl, gather_row(middle, 1), by_step, far_first)
    merged = multiply(trans, gather_row(summed), by_step)
    return core_send(merged)[None]


def solution(mesh):
    placed = (P("slab", "row", "col"), P("slab", "row", "col"), P("slab", "row", "col"))
    return jax.shard_map(
        on_device, mesh=mesh, in_specs=placed, out_specs=P("slab", "row", "col"), check_vma=False
    )
```

```python
import functools

import jax
import jax.numpy as jnp
from jax import lax
from jax.experimental import pallas as pl
from jax.experimental.pallas import tpu as pltpu
from jax.sharding import PartitionSpec as P

BF16 = jnp.bfloat16
F32 = jnp.float32


def after(array, *deps):
    return lax.optimization_barrier((array, *deps))[0]


def wait_all(arrays, gate):
    return [after(array, *gate) if gate else array for array in arrays]


def z_send(block, step, other=0):
    route = []
    for slab in range(4):
        for z in range(8):
            route.append((slab * 8 + z, (slab ^ other) * 8 + (z + step) % 8))
    return lax.ppermute(block, ("slab", "col"), route)


def send(block, step, side, other):
    route = []
    for slab in range(4):
        for row in range(8):
            x, y = row // 2, row % 2
            there = (x + step) % 4 * 2 + (y ^ side)
            route.append((slab * 8 + row, (slab ^ other) * 8 + there))
    return lax.ppermute(block, ("slab", "row"), route)


def core_send(block):
    return send(block, 0, 0, 1)


def gather_row(tile, here, other):
    half = tile.shape[0] // 2
    side = send(tile, 0, 1, other)
    below = send(tile, -1, 0, other)
    above = send(tile, 1, 0, other)
    above_side = send(side, 1, 0, 0)
    across = send(below, -1, 0, 0)
    below_side = send(below, 0, 1, 0)
    top = send(above_side[:half], 1, 0, 0)
    low = send(across[half:], 0, 1, 0)
    return [
        (0, 0, here),
        (1, 0, side),
        (2, 0, below),
        (6, 0, above),
        (7, 0, above_side),
        (4, 0, across),
        (3, 0, below_side),
        (5, 0, top),
        (5, half, low),
    ]


def pair_steps(tile, other, split):
    here = core_send(tile) if other else tile
    side = send(tile, 0, 1, other)
    gate = yield here, side
    (pair,) = wait_all([jnp.stack([here, side])], gate)
    below = send(pair, -1, 0, 0)
    above = send(pair, 1, 0, 0)
    gate = yield below, above
    below_on, above_on = wait_all((below, above), gate)
    if split:
        across = jnp.stack([send(below_on[0], -1, 0, 0), send(above_on[1], 1, 0, 0)])
    else:
        across = send(below_on, -1, 0, 0)
    yield (across,)
    yield jnp.concatenate([pair, below, across, above], axis=0)


def fold_tiles(beside, order, shots, *refs):
    *tiles, panel, sems = refs
    added = tiles[8:9] if beside else []
    outs = tiles[8 + len(added) :]
    tiles = tiles[:8]
    copies = []
    for index, tile in enumerate(tiles):
        copies.append(pltpu.make_async_copy(tile, panel.at[index], sems.at[index]))
        copies[-1].start()
    height = 128

    @pl.loop(0, outs[0].shape[0] // height)
    def _(chunk):
        rows = pl.ds(pl.multiple_of(chunk * height, height), height)
        total = None
        for step, tile in enumerate(tiles):
            term = jnp.dot(tile[rows, :], shots[order[step]], preferred_element_type=F32)
            total = term if total is None else total + term
        total = total.astype(outs[0].dtype)
        outs[0][rows, :] = total
        if beside:
            outs[1][0, rows, :] = total
            outs[1][1, rows, :] = added[0][rows, :]

    for copy in copies:
        copy.wait()


def multiply_tiles(tiles, shots, order, beside=None):
    rows, depth = tiles[0].shape
    count, _, columns = shots.shape
    extra = [] if beside is None else [beside]
    in_vmem = pl.BlockSpec(memory_space=pltpu.VMEM)
    *outs, panel = pl.pallas_call(
        functools.partial(fold_tiles, beside is not None),
        in_specs=[pl.BlockSpec(memory_space=pltpu.SMEM)] + [in_vmem] * (1 + count + len(extra)),
        out_specs=[in_vmem] * (1 + len(extra)) + [pl.BlockSpec(memory_space=pl.ANY)],
        out_shape=[jax.ShapeDtypeStruct((rows, columns), BF16)]
        + [jax.ShapeDtypeStruct((2, rows, columns), BF16) for _ in extra]
        + [jax.ShapeDtypeStruct((count, rows, depth), BF16)],
        scratch_shapes=[pltpu.SemaphoreType.DMA((count,))],
        compiler_params=pltpu.CompilerParams(vmem_limit_bytes=24 << 20),
        cost_estimate=pl.CostEstimate(
            flops=2 * count * rows * depth * columns,
            bytes_accessed=2 * count * depth * (rows + columns),
            transcendentals=0,
        ),
    )(order, shots, *tiles, *extra)
    return *outs, panel


def fold(pieces, order, operator, *refs):
    *shots, out = refs
    height = 128

    @pl.loop(0, out.shape[0] // height)
    def _(chunk):
        rows = pl.ds(pl.multiple_of(chunk * height, height), height)
        total = None
        for (place, start), shot in zip(pieces, shots):
            block = shot[0] if len(shot.shape) == 3 else shot[...]
            panel = operator[order[place], rows, start : start + block.shape[0]]
            term = jnp.dot(panel, block, preferred_element_type=F32)
            total = term if total is None else total + term
        if len(shots[0].shape) == 3:
            total = total + shots[0][1, rows, :].astype(F32)
        out[rows, :] = total.astype(out.dtype)


def multiply(operator, pieces, order):
    count, rows, depth = operator.shape
    shots = [piece[2] for piece in pieces]
    columns = shots[0].shape[-1]
    in_vmem = pl.BlockSpec(memory_space=pltpu.VMEM)
    return pl.pallas_call(
        functools.partial(fold, [piece[:2] for piece in pieces]),
        in_specs=[pl.BlockSpec(memory_space=pltpu.SMEM)] + [in_vmem] * (1 + len(shots)),
        out_specs=in_vmem,
        out_shape=jax.ShapeDtypeStruct((rows, columns), BF16),
        compiler_params=pltpu.CompilerParams(vmem_limit_bytes=24 << 20),
        cost_estimate=pl.CostEstimate(
            flops=2 * count * rows * depth * columns,
            bytes_accessed=2 * count * depth * (rows + columns),
            transcendentals=0,
        ),
    )(order, operator, *shots)


def on_device(reflection, transmission, shots):
    own_refl = reflection[0]
    own_trans = transmission[0]
    shot_tile = shots[0]
    row = lax.axis_index("row")
    x, y, z = row // 2, row % 2, lax.axis_index("col")
    place = jnp.arange(8, dtype=jnp.int32)
    block = (x + place // 2) % 4 * 2 + (y ^ place % 2)
    by_step = (block - z) % 8
    step_block = (place + z) % 8
    step_place = (step_block // 2 - x) % 4 * 2 + (step_block % 2 ^ y)
    t_down, t_up, r_down, r_up = {}, {}, {}, {}
    t_here = core_send(own_trans)
    t_down[1], t_up[1] = z_send(own_trans, -1, 1), z_send(own_trans, 1, 1)
    shot_ring = pair_steps(shot_tile, 1, False)
    gate = (*next(shot_ring), t_here)
    t_down[2] = z_send(after(t_down[1], *gate), -1)
    t_up[2] = z_send(after(t_up[1], *gate), 1)
    gate = next(shot_ring)
    t_down[3] = z_send(after(t_down[2], *gate), -1)
    t_up[3] = z_send(after(t_up[2], *gate), 1)
    gate = next(shot_ring)
    t_down[4] = z_send(after(t_down[3], *gate), -1)
    r_up[1] = z_send(after(own_refl, t_up[3], *gate), 1)
    incoming = after(next(shot_ring), r_up[1])
    tiles = [t_here, *(t_down[step] for step in (1, 2, 3, 4)), t_up[3], t_up[2], t_up[1]]
    first, trans = multiply_tiles(tiles, incoming, step_place)
    r_down[1] = z_send(after(own_refl, t_down[4]), -1)
    r_up[2] = z_send(r_up[1], 1)
    first_ring = pair_steps(first, 0, False)
    gate = next(first_ring)
    r_down[2] = z_send(after(r_down[1], *gate), -1)
    r_up[3] = z_send(after(r_up[2], *gate), 1)
    gate = first_ring.send((r_down[1], r_up[2]))
    r_down[3] = z_send(after(r_down[2], *gate), -1)
    r_up[4] = z_send(after(r_up[3], *gate), 1)
    first_ring.send((r_down[2], r_up[3]))
    passed = next(first_ring)
    tiles = [own_refl, *(r_down[step] for step in (1, 2, 3)), *(r_up[step] for step in (4, 3, 2, 1))]
    middle, pair, refl = multiply_tiles(tiles, passed, step_place, first)
    summed = multiply(refl, gather_row(middle, core_send(pair), 1), by_step)
    return multiply(trans, gather_row(summed, summed, 0), by_step)[None]


def solution(mesh):
    placed = (P("slab", "row", "col"), P("slab", "row", "col"), P("slab", "row", "col"))
    return jax.shard_map(
        on_device, mesh=mesh, in_specs=placed, out_specs=P("slab", "row", "col"), check_vma=False
    )
```

```python
import functools

import jax
import jax.numpy as jnp
from jax import lax
from jax.experimental import pallas as pl
from jax.experimental.pallas import tpu as pltpu
from jax.sharding import PartitionSpec as P

BF16 = jnp.bfloat16
F32 = jnp.float32


def after(array, *deps):
    return lax.optimization_barrier((array, *deps))[0]


def wait_all(arrays, gate):
    return [after(array, *gate) if gate else array for array in arrays]


def z_send(block, step, other=0):
    route = []
    for slab in range(4):
        for z in range(8):
            route.append((slab * 8 + z, (slab ^ other) * 8 + (z + step) % 8))
    return lax.ppermute(block, ("slab", "col"), route)


def send(block, step, side, other):
    route = []
    for slab in range(4):
        for row in range(8):
            x, y = row // 2, row % 2
            there = (x + step) % 4 * 2 + (y ^ side)
            route.append((slab * 8 + row, (slab ^ other) * 8 + there))
    return lax.ppermute(block, ("slab", "row"), route)


def core_send(block):
    return send(block, 0, 0, 1)


def gather_row(tile, here, other):
    half = tile.shape[0] // 2
    side = send(tile, 0, 1, other)
    below = send(tile, -1, 0, other)
    above = send(tile, 1, 0, other)
    side_on, below_on = wait_all((side, below), (above,))
    above_side = send(side_on, 1, 0, 0)
    across = send(below_on, -1, 0, 0)
    below_side = send(below_on, 0, 1, 0)
    top = send(above_side[:half], 1, 0, 0)
    low = send(across[half:], 0, 1, 0)
    return [
        (0, 0, here),
        (1, 0, side),
        (2, 0, below),
        (6, 0, above),
        (7, 0, above_side),
        (4, 0, across),
        (3, 0, below_side),
        (5, 0, top),
        (5, half, low),
    ]


def pair_steps(tile, other, split):
    here = core_send(tile) if other else tile
    side = send(tile, 0, 1, other)
    gate = yield here, side
    (pair,) = wait_all([jnp.stack([here, side])], gate)
    below = send(pair, -1, 0, 0)
    above = send(pair, 1, 0, 0)
    gate = yield below, above
    below_on, above_on = wait_all((below, above), gate)
    if split:
        across = jnp.stack([send(below_on[0], -1, 0, 0), send(above_on[1], 1, 0, 0)])
    else:
        across = send(below_on, -1, 0, 0)
    yield (across,)
    yield jnp.concatenate([pair, below, across, above], axis=0)


def fold_tiles(beside, order, shots, *refs):
    *tiles, panel, sems = refs
    added = tiles[8:9] if beside else []
    outs = tiles[8 + len(added) :]
    tiles = tiles[:8]
    copies = []
    for index, tile in enumerate(tiles):
        copies.append(pltpu.make_async_copy(tile, panel.at[index], sems.at[index]))
        copies[-1].start()
    height = 256

    @pl.loop(0, outs[0].shape[0] // height)
    def _(chunk):
        rows = pl.ds(pl.multiple_of(chunk * height, height), height)
        total = None
        for step, tile in enumerate(tiles):
            term = jnp.dot(tile[rows, :], shots[order[step]], preferred_element_type=F32)
            total = term if total is None else total + term
        total = total.astype(outs[0].dtype)
        outs[0][rows, :] = total
        if beside:
            outs[1][0, rows, :] = total
            outs[1][1, rows, :] = added[0][rows, :]

    for copy in copies:
        copy.wait()


def multiply_tiles(tiles, shots, order, beside=None):
    rows, depth = tiles[0].shape
    count, _, columns = shots.shape
    extra = [] if beside is None else [beside]
    in_vmem = pl.BlockSpec(memory_space=pltpu.VMEM)
    *outs, panel = pl.pallas_call(
        functools.partial(fold_tiles, beside is not None),
        in_specs=[pl.BlockSpec(memory_space=pltpu.SMEM)] + [in_vmem] * (1 + count + len(extra)),
        out_specs=[in_vmem] * (1 + len(extra)) + [pl.BlockSpec(memory_space=pl.ANY)],
        out_shape=[jax.ShapeDtypeStruct((rows, columns), BF16)]
        + [jax.ShapeDtypeStruct((2, rows, columns), BF16) for _ in extra]
        + [jax.ShapeDtypeStruct((count, rows, depth), BF16)],
        scratch_shapes=[pltpu.SemaphoreType.DMA((count,))],
        compiler_params=pltpu.CompilerParams(vmem_limit_bytes=24 << 20),
        cost_estimate=pl.CostEstimate(
            flops=2 * count * rows * depth * columns,
            bytes_accessed=2 * count * depth * (rows + columns),
            transcendentals=0,
        ),
    )(order, shots, *tiles, *extra)
    return *outs, panel


def fold(pieces, added, order, operator, *refs):
    *shots, out = refs
    height = 256

    @pl.loop(0, out.shape[0] // height)
    def _(chunk):
        rows = pl.ds(pl.multiple_of(chunk * height, height), height)
        total = shots[-1][rows, :] if added else None
        for (place, start), shot in zip(pieces, shots):
            block = shot[0] if len(shot.shape) == 3 else shot[...]
            panel = operator[order[place], rows, start : start + block.shape[0]]
            term = jnp.dot(panel, block, preferred_element_type=F32)
            total = term if total is None else total + term
        if len(shots[0].shape) == 3:
            total = total + shots[0][1, rows, :].astype(F32)
        out[rows, :] = total.astype(out.dtype)


def multiply_some(operator, pieces, order, dtype, added):
    _, rows, _ = operator.shape
    shots = [piece[2] for piece in pieces]
    columns = shots[0].shape[-1]
    depth = sum(shot.shape[-2] for shot in shots)
    in_vmem = pl.BlockSpec(memory_space=pltpu.VMEM)
    return pl.pallas_call(
        functools.partial(fold, [piece[:2] for piece in pieces], len(added) > 0),
        in_specs=[pl.BlockSpec(memory_space=pltpu.SMEM)] + [in_vmem] * (1 + len(shots) + len(added)),
        out_specs=in_vmem,
        out_shape=jax.ShapeDtypeStruct((rows, columns), dtype),
        compiler_params=pltpu.CompilerParams(vmem_limit_bytes=24 << 20),
        cost_estimate=pl.CostEstimate(
            flops=2 * rows * depth * columns,
            bytes_accessed=2 * depth * (rows + columns),
            transcendentals=0,
        ),
    )(order, operator, *shots, *added)


def multiply(operator, pieces, order):
    early = multiply_some(operator, pieces[:7], order, F32, ())
    return multiply_some(operator, pieces[7:], order, BF16, (early,))


def on_device(reflection, transmission, shots):
    own_refl = reflection[0]
    own_trans = transmission[0]
    shot_tile = shots[0]
    row = lax.axis_index("row")
    x, y, z = row // 2, row % 2, lax.axis_index("col")
    place = jnp.arange(8, dtype=jnp.int32)
    block = (x + place // 2) % 4 * 2 + (y ^ place % 2)
    by_step = (block - z) % 8
    step_block = (place + z) % 8
    step_place = (step_block // 2 - x) % 4 * 2 + (step_block % 2 ^ y)
    t_down, t_up, r_down, r_up = {}, {}, {}, {}
    t_here = core_send(own_trans)
    t_down[1], t_up[1] = z_send(own_trans, -1, 1), z_send(own_trans, 1, 1)
    shot_ring = pair_steps(shot_tile, 1, False)
    gate = (*next(shot_ring), t_here)
    t_down[2] = z_send(after(t_down[1], *gate), -1)
    t_up[2] = z_send(after(t_up[1], *gate), 1)
    gate = next(shot_ring)
    t_down[3] = z_send(after(t_down[2], *gate), -1)
    t_up[3] = z_send(after(t_up[2], *gate), 1)
    gate = next(shot_ring)
    t_down[4] = z_send(after(t_down[3], *gate), -1)
    r_up[1] = z_send(after(own_refl, t_up[3], *gate), 1)
    incoming = after(next(shot_ring), r_up[1])
    tiles = [t_here, *(t_down[step] for step in (1, 2, 3, 4)), t_up[3], t_up[2], t_up[1]]
    first, trans = multiply_tiles(tiles, incoming, step_place)
    r_down[1] = z_send(after(own_refl, t_down[4]), -1)
    r_up[2] = z_send(r_up[1], 1)
    first_ring = pair_steps(first, 0, False)
    gate = next(first_ring)
    r_down[2] = z_send(after(r_down[1], *gate), -1)
    r_up[3] = z_send(after(r_up[2], *gate), 1)
    gate = first_ring.send((r_down[1], r_up[2]))
    r_down[3] = z_send(after(r_down[2], *gate), -1)
    r_up[4] = z_send(after(r_up[3], *gate), 1)
    first_ring.send((r_down[2], r_up[3]))
    passed = next(first_ring)
    tiles = [own_refl, *(r_down[step] for step in (1, 2, 3)), *(r_up[step] for step in (4, 3, 2, 1))]
    middle, pair, refl = multiply_tiles(tiles, passed, step_place, first)
    summed = multiply(refl, gather_row(middle, core_send(pair), 1), by_step)
    return multiply(trans, gather_row(summed, summed, 0), by_step)[None]


def solution(mesh):
    placed = (P("slab", "row", "col"), P("slab", "row", "col"), P("slab", "row", "col"))
    return jax.shard_map(
        on_device, mesh=mesh, in_specs=placed, out_specs=P("slab", "row", "col"), check_vma=False
    )
```

```python
import functools

import jax
import jax.numpy as jnp
from jax import lax
from jax.experimental import pallas as pl
from jax.experimental.pallas import tpu as pltpu
from jax.sharding import PartitionSpec as P

BF16 = jnp.bfloat16
F32 = jnp.float32


def after(array, *deps):
    return lax.optimization_barrier((array, *deps))[0]


def wait_all(arrays, gate):
    return [after(array, *gate) if gate else array for array in arrays]


def z_send(block, step, other=0):
    route = []
    for slab in range(4):
        for z in range(8):
            route.append((slab * 8 + z, (slab ^ other) * 8 + (z + step) % 8))
    return lax.ppermute(block, ("slab", "col"), route)


def row_swap(block, flip, other=0):
    route = []
    for slab in range(4):
        for row in range(8):
            route.append((slab * 8 + row, (slab ^ other) * 8 + (row ^ flip)))
    return lax.ppermute(block, ("slab", "row"), route)


def core_swap(block):
    return row_swap(block, 0, 1)


def gather_row(tile, here, other):
    half = tile.shape[0] // 2
    near = row_swap(tile, 2, other)
    far = row_swap(tile, 6, other)
    side = row_swap(tile, 1, other)
    near_side = row_swap(side, 2)
    across = row_swap(near, 6)
    far_side = row_swap(far, 1)
    top = row_swap(far_side[:half], 2)
    low = row_swap(across[half:], 1)
    return [
        (0, 0, here),
        (1, 0, side),
        (2, 0, near),
        (6, 0, far),
        (3, 0, near_side),
        (4, 0, across),
        (7, 0, far_side),
        (5, 0, top),
        (5, half, low),
    ]


def pair_steps(tile, other, split):
    here = core_swap(tile) if other else tile
    side = row_swap(tile, 1, other)
    gate = yield here, side
    (pair,) = wait_all([jnp.stack([here, side])], gate)
    near = row_swap(pair, 2)
    far = row_swap(pair, 6)
    gate = yield near, far
    near_on, far_on = wait_all((near, far), gate)
    if split:
        across = jnp.stack([row_swap(far_on[0], 2), row_swap(near_on[1], 6)])
    else:
        across = row_swap(far_on, 2)
    yield (across,)
    yield jnp.concatenate([pair, near, across, far], axis=0)


def fold_tiles(steps, beside, order, shots, *refs):
    count = len(steps)
    tiles, refs = refs[:count], refs[count:]
    height = 256
    if beside:
        early, held, out, both = refs
    else:
        (out,) = refs

    @pl.loop(0, out.shape[0] // height)
    def _(chunk):
        rows = pl.ds(pl.multiple_of(chunk * height, height), height)
        total = early[rows, :] if beside else None
        for step, tile in zip(steps, tiles):
            term = jnp.dot(tile[rows, :], shots[order[step]], preferred_element_type=F32)
            total = term if total is None else total + term
        total = total.astype(out.dtype)
        out[rows, :] = total
        if beside:
            both[0, rows, :] = total
            both[1, rows, :] = held[rows, :]


def multiply_tiles(tiles, shots, order, dtype, beside=()):
    steps = tuple(tiles)
    rows, depth = tiles[steps[0]].shape
    columns = shots.shape[2]
    in_vmem = pl.BlockSpec(memory_space=pltpu.VMEM)
    out = jax.ShapeDtypeStruct((rows, columns), dtype)
    pair = jax.ShapeDtypeStruct((2, rows, columns), dtype)
    return pl.pallas_call(
        functools.partial(fold_tiles, steps, len(beside) > 0),
        in_specs=[pl.BlockSpec(memory_space=pltpu.SMEM)]
        + [in_vmem] * (1 + len(steps) + len(beside)),
        out_specs=[in_vmem] * 2 if beside else in_vmem,
        out_shape=[out, pair] if beside else out,
        compiler_params=pltpu.CompilerParams(vmem_limit_bytes=24 << 20),
        cost_estimate=pl.CostEstimate(
            flops=2 * len(steps) * rows * depth * columns,
            bytes_accessed=2 * len(steps) * depth * (rows + columns),
            transcendentals=0,
        ),
    )(order, shots, *tiles.values(), *beside)


def panel_of(tiles):
    count = len(tiles)
    rows, depth = tiles[0].shape

    def kernel(*refs):
        *parts, panel, sems = refs
        copies = []
        for step in range(count):
            copies.append(pltpu.make_async_copy(parts[step], panel.at[step], sems.at[step]))
            copies[-1].start()
        for copy in copies:
            copy.wait()

    return pl.pallas_call(
        kernel,
        in_specs=[pl.BlockSpec(memory_space=pl.ANY)] * count,
        out_specs=pl.BlockSpec(memory_space=pl.ANY),
        out_shape=jax.ShapeDtypeStruct((count, rows, depth), BF16),
        scratch_shapes=[pltpu.SemaphoreType.DMA((count,))],
        compiler_params=pltpu.CompilerParams(vmem_limit_bytes=1 << 20),
    )(*(tiles[step] for step in range(count)))


def fold(pieces, added, order, operator, *refs):
    *shots, out = refs
    height = 256

    @pl.loop(0, out.shape[0] // height)
    def _(chunk):
        rows = pl.ds(pl.multiple_of(chunk * height, height), height)
        total = shots[-1][rows, :] if added else None
        for (place, start), shot in zip(pieces, shots):
            block = shot[0] if len(shot.shape) == 3 else shot[...]
            panel = operator[order[place], rows, start : start + block.shape[0]]
            term = jnp.dot(panel, block, preferred_element_type=F32)
            total = term if total is None else total + term
        if len(shots[0].shape) == 3:
            total = total + shots[0][1, rows, :].astype(F32)
        out[rows, :] = total.astype(out.dtype)


def multiply_some(operator, pieces, order, dtype, added):
    _, rows, _ = operator.shape
    shots = [piece[2] for piece in pieces]
    columns = shots[0].shape[-1]
    depth = sum(shot.shape[-2] for shot in shots)
    in_vmem = pl.BlockSpec(memory_space=pltpu.VMEM)
    return pl.pallas_call(
        functools.partial(fold, [piece[:2] for piece in pieces], len(added) > 0),
        in_specs=[pl.BlockSpec(memory_space=pltpu.SMEM)] + [in_vmem] * (1 + len(shots) + len(added)),
        out_specs=in_vmem,
        out_shape=jax.ShapeDtypeStruct((rows, columns), dtype),
        compiler_params=pltpu.CompilerParams(vmem_limit_bytes=24 << 20),
        cost_estimate=pl.CostEstimate(
            flops=2 * rows * depth * columns,
            bytes_accessed=2 * depth * (rows + columns),
            transcendentals=0,
        ),
    )(order, operator, *shots, *added)


def multiply(operator, pieces, order):
    early = multiply_some(operator, pieces[:7], order, F32, ())
    return multiply_some(operator, pieces[7:], order, BF16, (early,))


def on_device(reflection, transmission, shots):
    own_refl = reflection[0]
    own_trans = transmission[0]
    shot_tile = shots[0]
    row, z = lax.axis_index("row"), lax.axis_index("col")
    place = jnp.arange(8, dtype=jnp.int32)
    by_step = ((row ^ place) - z + 8) % 8
    step_place = row ^ (z + place) % 8

    t_down, t_up, r_down, r_up = {}, {}, {}, {}
    t_here = core_swap(own_trans)
    t_down[1], t_up[1] = z_send(own_trans, -1, 1), z_send(own_trans, 1, 1)
    shot_ring = pair_steps(shot_tile, 1, False)
    gate = (*next(shot_ring), t_here)
    t_down[2] = z_send(after(t_down[1], *gate), -1)
    t_up[2] = z_send(after(t_up[1], *gate), 1)
    gate = next(shot_ring)
    t_down[3] = z_send(after(t_down[2], *gate), -1)
    t_up[3] = z_send(after(t_up[2], *gate), 1)
    gate = next(shot_ring)
    t_down[4] = z_send(after(t_down[3], *gate), -1)
    r_up[1] = z_send(after(own_refl, t_up[3], *gate), 1)
    incoming = after(next(shot_ring), r_up[1])
    tiles = {0: t_here, **t_down, 5: t_up[3], 6: t_up[2], 7: t_up[1]}
    first = multiply_tiles(tiles, incoming, step_place, BF16)
    trans = tiles
    r_down[1] = z_send(after(own_refl, t_down[4]), -1)
    r_up[2] = z_send(r_up[1], 1)
    first_ring = pair_steps(first, 0, True)
    gate = next(first_ring)
    r_down[2] = z_send(after(r_down[1], *gate), -1)
    r_up[3] = z_send(after(r_up[2], *gate), 1)
    first_ring.send((r_down[1], r_up[2]))
    r_down[3] = z_send(r_down[2], -1)
    r_up[4] = z_send(r_up[3], 1)
    first_ring.send((r_down[2], r_up[3]))
    passed = next(first_ring)
    tiles = {0: own_refl, 1: r_down[1], 2: r_down[2], 5: r_up[3], 6: r_up[2], 7: r_up[1]}
    early = multiply_tiles(tiles, passed, step_place, F32)
    late = {3: r_down[3], 4: r_up[4]}
    middle, pair = multiply_tiles(late, passed, step_place, BF16, (early, first))
    refl = panel_of({**tiles, **late})
    summed = multiply(refl, gather_row(middle, core_swap(pair), 1), by_step)
    return multiply(panel_of(trans), gather_row(summed, summed, 0), by_step)[None]


def solution(mesh):
    placed = (P("slab", "row", "col"), P("slab", "row", "col"), P("slab", "row", "col"))
    return jax.shard_map(
        on_device, mesh=mesh, in_specs=placed, out_specs=P("slab", "row", "col"), check_vma=False
    )
```

```python
import functools

import jax
import jax.numpy as jnp
from jax import lax
from jax.experimental import pallas as pl
from jax.experimental.pallas import tpu as pltpu
from jax.sharding import PartitionSpec as P

BF16 = jnp.bfloat16
F32 = jnp.float32


def after(array, *deps):
    return lax.optimization_barrier((array, *deps))[0]


def wait_all(arrays, gate):
    return [after(array, *gate) if gate else array for array in arrays]


def z_send(block, step, other=0):
    route = []
    for slab in range(4):
        for z in range(8):
            route.append((slab * 8 + z, (slab ^ other) * 8 + (z + step) % 8))
    return lax.ppermute(block, ("slab", "col"), route)


def row_swap(block, flip, other=0):
    route = []
    for slab in range(4):
        for row in range(8):
            route.append((slab * 8 + row, (slab ^ other) * 8 + (row ^ flip)))
    return lax.ppermute(block, ("slab", "row"), route)


def core_swap(block):
    return row_swap(block, 0, 1)


def gather_row(tile, here, other):
    half = tile.shape[0] // 2
    near = row_swap(tile, 2, other)
    far = row_swap(tile, 6, other)
    side = row_swap(tile, 1, other)
    near_side = row_swap(side, 2)
    across = row_swap(near, 6)
    far_side = row_swap(far, 1)
    top = row_swap(far_side[:half], 2)
    low = row_swap(across[half:], 1)
    return [
        (0, 0, here),
        (1, 0, side),
        (2, 0, near),
        (6, 0, far),
        (3, 0, near_side),
        (4, 0, across),
        (7, 0, far_side),
        (5, 0, top),
        (5, half, low),
    ]


def pair_steps(tile, other, split):
    here = core_swap(tile) if other else tile
    side = row_swap(tile, 1, other)
    gate = yield here, side
    (pair,) = wait_all([jnp.stack([here, side])], gate)
    near = row_swap(pair, 2)
    far = row_swap(pair, 6)
    gate = yield near, far
    near_on, far_on = wait_all((near, far), gate)
    if split:
        across = jnp.stack([row_swap(far_on[0], 2), row_swap(near_on[1], 6)])
    else:
        across = row_swap(far_on, 2)
    yield (across,)
    yield jnp.concatenate([pair, near, across, far], axis=0)


def fold_tiles(steps, beside, order, shots, *refs):
    count = len(steps)
    tiles, refs = refs[:count], refs[count:]
    height = 256
    if beside:
        early, held, out, both = refs
    else:
        (out,) = refs

    @pl.loop(0, out.shape[0] // height)
    def _(chunk):
        rows = pl.ds(pl.multiple_of(chunk * height, height), height)
        total = early[rows, :] if beside else None
        for step, tile in zip(steps, tiles):
            term = jnp.dot(tile[rows, :], shots[order[step]], preferred_element_type=F32)
            total = term if total is None else total + term
        total = total.astype(out.dtype)
        out[rows, :] = total
        if beside:
            both[0, rows, :] = total
            both[1, rows, :] = held[rows, :]


def multiply_tiles(tiles, shots, order, dtype, beside=()):
    steps = tuple(tiles)
    rows, depth = tiles[steps[0]].shape
    columns = shots.shape[2]
    in_vmem = pl.BlockSpec(memory_space=pltpu.VMEM)
    out = jax.ShapeDtypeStruct((rows, columns), dtype)
    pair = jax.ShapeDtypeStruct((2, rows, columns), dtype)
    return pl.pallas_call(
        functools.partial(fold_tiles, steps, len(beside) > 0),
        in_specs=[pl.BlockSpec(memory_space=pltpu.SMEM)]
        + [in_vmem] * (1 + len(steps) + len(beside)),
        out_specs=[in_vmem] * 2 if beside else in_vmem,
        out_shape=[out, pair] if beside else out,
        compiler_params=pltpu.CompilerParams(vmem_limit_bytes=24 << 20),
        cost_estimate=pl.CostEstimate(
            flops=2 * len(steps) * rows * depth * columns,
            bytes_accessed=2 * len(steps) * depth * (rows + columns),
            transcendentals=0,
        ),
    )(order, shots, *tiles.values(), *beside)


def panel_of(tiles):
    count = len(tiles)
    rows, depth = tiles[0].shape

    def kernel(*refs):
        *parts, panel, sems = refs
        copies = []
        for step in range(count):
            copies.append(pltpu.make_async_copy(parts[step], panel.at[step], sems.at[step]))
            copies[-1].start()
        for copy in copies:
            copy.wait()

    return pl.pallas_call(
        kernel,
        in_specs=[pl.BlockSpec(memory_space=pl.ANY)] * count,
        out_specs=pl.BlockSpec(memory_space=pl.ANY),
        out_shape=jax.ShapeDtypeStruct((count, rows, depth), BF16),
        scratch_shapes=[pltpu.SemaphoreType.DMA((count,))],
        compiler_params=pltpu.CompilerParams(vmem_limit_bytes=1 << 20),
    )(*(tiles[step] for step in range(count)))


def fold(pieces, added, order, operator, *refs):
    *shots, out = refs
    height = 256

    @pl.loop(0, out.shape[0] // height)
    def _(chunk):
        rows = pl.ds(pl.multiple_of(chunk * height, height), height)
        total = shots[-1][rows, :] if added else None
        for (place, start), shot in zip(pieces, shots):
            block = shot[0] if len(shot.shape) == 3 else shot[...]
            panel = operator[order[place], rows, start : start + block.shape[0]]
            term = jnp.dot(panel, block, preferred_element_type=F32)
            total = term if total is None else total + term
        if len(shots[0].shape) == 3:
            total = total + shots[0][1, rows, :].astype(F32)
        out[rows, :] = total.astype(out.dtype)


def multiply_some(operator, pieces, order, dtype, added):
    _, rows, _ = operator.shape
    shots = [piece[2] for piece in pieces]
    columns = shots[0].shape[-1]
    depth = sum(shot.shape[-2] for shot in shots)
    in_vmem = pl.BlockSpec(memory_space=pltpu.VMEM)
    return pl.pallas_call(
        functools.partial(fold, [piece[:2] for piece in pieces], len(added) > 0),
        in_specs=[pl.BlockSpec(memory_space=pltpu.SMEM)] + [in_vmem] * (1 + len(shots) + len(added)),
        out_specs=in_vmem,
        out_shape=jax.ShapeDtypeStruct((rows, columns), dtype),
        compiler_params=pltpu.CompilerParams(vmem_limit_bytes=24 << 20),
        cost_estimate=pl.CostEstimate(
            flops=2 * rows * depth * columns,
            bytes_accessed=2 * depth * (rows + columns),
            transcendentals=0,
        ),
    )(order, operator, *shots, *added)


def multiply(operator, pieces, order):
    early = multiply_some(operator, pieces[:7], order, F32, ())
    return multiply_some(operator, pieces[7:], order, BF16, (early,))


def on_device(reflection, transmission, shots):
    own_refl = reflection[0]
    own_trans = transmission[0]
    shot_tile = shots[0]
    row, z = lax.axis_index("row"), lax.axis_index("col")
    place = jnp.arange(8, dtype=jnp.int32)
    by_step = ((row ^ place) - z + 8) % 8
    step_place = row ^ (z + place) % 8

    t_down, t_up, r_down, r_up = {}, {}, {}, {}
    t_here = core_swap(own_trans)
    t_down[1], t_up[1] = z_send(own_trans, -1, 1), z_send(own_trans, 1, 1)
    shot_ring = pair_steps(shot_tile, 1, False)
    gate = (*next(shot_ring), t_here)
    t_down[2] = z_send(after(t_down[1], *gate), -1)
    t_up[2] = z_send(after(t_up[1], *gate), 1)
    gate = next(shot_ring)
    t_down[3] = z_send(after(t_down[2], *gate), -1)
    t_up[3] = z_send(after(t_up[2], *gate), 1)
    gate = next(shot_ring)
    t_down[4] = z_send(after(t_down[3], *gate), -1)
    r_up[1] = z_send(after(own_refl, t_up[3], *gate), 1)
    incoming = after(next(shot_ring), r_up[1])
    tiles = {0: t_here, **t_down, 5: t_up[3], 6: t_up[2], 7: t_up[1]}
    first = multiply_tiles(tiles, incoming, step_place, BF16)
    trans = tiles
    r_down[1] = z_send(after(own_refl, t_down[4]), -1)
    r_up[2] = z_send(r_up[1], 1)
    first_ring = pair_steps(first, 0, True)
    gate = next(first_ring)
    r_down[2] = z_send(after(r_down[1], *gate), -1)
    r_up[3] = z_send(after(r_up[2], *gate), 1)
    first_ring.send((r_down[1], r_up[2]))
    r_down[3] = z_send(r_down[2], -1)
    r_up[4] = z_send(r_up[3], 1)
    next(first_ring)
    passed = next(first_ring)
    tiles = {0: own_refl, 1: r_down[1], 2: r_down[2], 5: r_up[3], 6: r_up[2], 7: r_up[1]}
    early = multiply_tiles(tiles, passed, step_place, F32)
    late = {3: r_down[3], 4: r_up[4]}
    middle, pair = multiply_tiles(late, passed, step_place, BF16, (early, first))
    refl = panel_of({**tiles, **late})
    summed = multiply(refl, gather_row(middle, core_swap(pair), 1), by_step)
    return multiply(panel_of(trans), gather_row(summed, summed, 0), by_step)[None]


def solution(mesh):
    placed = (P("slab", "row", "col"), P("slab", "row", "col"), P("slab", "row", "col"))
    return jax.shard_map(
        on_device, mesh=mesh, in_specs=placed, out_specs=P("slab", "row", "col"), check_vma=False
    )
```

```python
import functools

import jax
import jax.numpy as jnp
from jax import lax
from jax.experimental import pallas as pl
from jax.experimental.pallas import tpu as pltpu
from jax.sharding import PartitionSpec as P

BF16 = jnp.bfloat16
F32 = jnp.float32


def after(array, *deps):
    return lax.optimization_barrier((array, *deps))[0]


def wait_all(arrays, gate):
    return [after(array, *gate) if gate else array for array in arrays]


def z_send(block, step, other=0):
    route = []
    for slab in range(4):
        for z in range(8):
            route.append((slab * 8 + z, (slab ^ other) * 8 + (z + step) % 8))
    return lax.ppermute(block, ("slab", "col"), route)


def row_swap(block, flip, other=0):
    route = []
    for slab in range(4):
        for row in range(8):
            route.append((slab * 8 + row, (slab ^ other) * 8 + (row ^ flip)))
    return lax.ppermute(block, ("slab", "row"), route)


def core_swap(block):
    return row_swap(block, 0, 1)


def gather_row(tile, here, other):
    half = tile.shape[0] // 2
    near = row_swap(tile, 2, other)
    far = row_swap(tile, 6, other)
    side = row_swap(tile, 1, other)
    near_side = row_swap(side, 2)
    across = row_swap(near, 6)
    far_side = row_swap(far, 1)
    top = row_swap(far_side[:half], 2)
    low = row_swap(across[half:], 1)
    return [
        (0, 0, here),
        (1, 0, side),
        (2, 0, near),
        (6, 0, far),
        (3, 0, near_side),
        (4, 0, across),
        (7, 0, far_side),
        (5, 0, top),
        (5, half, low),
    ]


def pair_steps(tile, other, split):
    here = core_swap(tile) if other else tile
    side = row_swap(tile, 1, other)
    gate = yield here, side
    (pair,) = wait_all([jnp.stack([here, side])], gate)
    near = row_swap(pair, 2)
    far = row_swap(pair, 6)
    gate = yield near, far
    near_on, far_on = wait_all((near, far), gate)
    if split:
        across = jnp.stack([row_swap(far_on[0], 2), row_swap(near_on[1], 6)])
    else:
        across = row_swap(far_on, 2)
    yield (across,)
    yield jnp.concatenate([pair, near, across, far], axis=0)


def fold_tiles(steps, beside, order, shots, *refs):
    count = len(steps)
    tiles, refs = refs[:count], refs[count:]
    height = 256
    if beside == 2:
        early, held, out, both = refs
    elif beside == 1:
        early, out = refs
    else:
        (out,) = refs

    @pl.loop(0, out.shape[0] // height)
    def _(chunk):
        rows = pl.ds(pl.multiple_of(chunk * height, height), height)
        total = early[rows, :] if beside else None
        for step, tile in zip(steps, tiles):
            term = jnp.dot(tile[rows, :], shots[order[step]], preferred_element_type=F32)
            total = term if total is None else total + term
        total = total.astype(out.dtype)
        out[rows, :] = total
        if beside == 2:
            both[0, rows, :] = total
            both[1, rows, :] = held[rows, :]


def multiply_tiles(tiles, shots, order, dtype, beside=()):
    steps = tuple(tiles)
    rows, depth = tiles[steps[0]].shape
    columns = shots.shape[2]
    in_vmem = pl.BlockSpec(memory_space=pltpu.VMEM)
    out = jax.ShapeDtypeStruct((rows, columns), dtype)
    pair = jax.ShapeDtypeStruct((2, rows, columns), dtype)
    return pl.pallas_call(
        functools.partial(fold_tiles, steps, len(beside)),
        in_specs=[pl.BlockSpec(memory_space=pltpu.SMEM)]
        + [in_vmem] * (1 + len(steps) + len(beside)),
        out_specs=[in_vmem] * 2 if len(beside) == 2 else in_vmem,
        out_shape=[out, pair] if len(beside) == 2 else out,
        compiler_params=pltpu.CompilerParams(vmem_limit_bytes=24 << 20),
        cost_estimate=pl.CostEstimate(
            flops=2 * len(steps) * rows * depth * columns,
            bytes_accessed=2 * len(steps) * depth * (rows + columns),
            transcendentals=0,
        ),
    )(order, shots, *tiles.values(), *beside)


def panel_of(tiles):
    count = len(tiles)
    rows, depth = tiles[0].shape

    def kernel(*refs):
        *parts, panel, sems = refs
        copies = []
        for step in range(count):
            copies.append(pltpu.make_async_copy(parts[step], panel.at[step], sems.at[step]))
            copies[-1].start()
        for copy in copies:
            copy.wait()

    return pl.pallas_call(
        kernel,
        in_specs=[pl.BlockSpec(memory_space=pl.ANY)] * count,
        out_specs=pl.BlockSpec(memory_space=pl.ANY),
        out_shape=jax.ShapeDtypeStruct((count, rows, depth), BF16),
        scratch_shapes=[pltpu.SemaphoreType.DMA((count,))],
        compiler_params=pltpu.CompilerParams(vmem_limit_bytes=1 << 20),
    )(*(tiles[step] for step in range(count)))


def fold(pieces, added, order, operator, *refs):
    *shots, out = refs
    height = 256

    @pl.loop(0, out.shape[0] // height)
    def _(chunk):
        rows = pl.ds(pl.multiple_of(chunk * height, height), height)
        total = shots[-1][rows, :] if added else None
        for (place, start), shot in zip(pieces, shots):
            block = shot[0] if len(shot.shape) == 3 else shot[...]
            panel = operator[order[place], rows, start : start + block.shape[0]]
            term = jnp.dot(panel, block, preferred_element_type=F32)
            total = term if total is None else total + term
        if len(shots[0].shape) == 3:
            total = total + shots[0][1, rows, :].astype(F32)
        out[rows, :] = total.astype(out.dtype)


def multiply_some(operator, pieces, order, dtype, added):
    _, rows, _ = operator.shape
    shots = [piece[2] for piece in pieces]
    columns = shots[0].shape[-1]
    depth = sum(shot.shape[-2] for shot in shots)
    in_vmem = pl.BlockSpec(memory_space=pltpu.VMEM)
    return pl.pallas_call(
        functools.partial(fold, [piece[:2] for piece in pieces], len(added) > 0),
        in_specs=[pl.BlockSpec(memory_space=pltpu.SMEM)] + [in_vmem] * (1 + len(shots) + len(added)),
        out_specs=in_vmem,
        out_shape=jax.ShapeDtypeStruct((rows, columns), dtype),
        compiler_params=pltpu.CompilerParams(vmem_limit_bytes=24 << 20),
        cost_estimate=pl.CostEstimate(
            flops=2 * rows * depth * columns,
            bytes_accessed=2 * depth * (rows + columns),
            transcendentals=0,
        ),
    )(order, operator, *shots, *added)


def multiply(operator, pieces, order):
    early = multiply_some(operator, pieces[:7], order, F32, ())
    return multiply_some(operator, pieces[7:], order, BF16, (early,))


def on_device(reflection, transmission, shots):
    own_refl = reflection[0]
    own_trans = transmission[0]
    shot_tile = shots[0]
    row, z = lax.axis_index("row"), lax.axis_index("col")
    place = jnp.arange(8, dtype=jnp.int32)
    by_step = ((row ^ place) - z + 8) % 8
    step_place = row ^ (z + place) % 8

    t_down, t_up, r_down, r_up = {}, {}, {}, {}
    t_here = core_swap(own_trans)
    t_down[1], t_up[1] = z_send(own_trans, -1, 1), z_send(own_trans, 1, 1)
    shot_ring = pair_steps(shot_tile, 1, False)
    gate = (*next(shot_ring), t_here)
    t_down[2] = z_send(after(t_down[1], *gate), -1)
    t_up[2] = z_send(after(t_up[1], *gate), 1)
    gate = next(shot_ring)
    t_down[3] = z_send(after(t_down[2], *gate), -1)
    t_up[3] = z_send(after(t_up[2], *gate), 1)
    gate = next(shot_ring)
    t_down[4] = z_send(after(t_down[3], *gate), -1)
    r_up[1] = z_send(after(own_refl, t_up[3], *gate), 1)
    incoming = next(shot_ring)
    tiles = {0: t_here, **t_down, 5: t_up[3], 6: t_up[2], 7: t_up[1]}
    soon = {step: tiles[step] for step in tiles if step != 4}
    early = multiply_tiles(soon, incoming, step_place, F32)
    late = {4: after(t_down[4], r_up[1])}
    first = multiply_tiles(late, incoming, step_place, BF16, (early,))
    trans = tiles
    r_down[1] = z_send(after(own_refl, t_down[4]), -1)
    r_up[2] = z_send(r_up[1], 1)
    first_ring = pair_steps(first, 0, True)
    gate = next(first_ring)
    r_down[2] = z_send(after(r_down[1], *gate), -1)
    r_up[3] = z_send(after(r_up[2], *gate), 1)
    next(first_ring)
    r_down[3] = z_send(r_down[2], -1)
    r_up[4] = z_send(r_up[3], 1)
    first_ring.send((r_down[1], r_up[2]))
    passed = next(first_ring)
    tiles = {0: own_refl, 1: r_down[1], 2: r_down[2], 5: r_up[3], 6: r_up[2], 7: r_up[1]}
    early = multiply_tiles(tiles, passed, step_place, F32)
    late = {3: r_down[3], 4: r_up[4]}
    middle, pair = multiply_tiles(late, passed, step_place, BF16, (early, first))
    refl = panel_of({**tiles, **late})
    summed = multiply(refl, gather_row(middle, core_swap(pair), 1), by_step)
    return multiply(panel_of(trans), gather_row(summed, summed, 0), by_step)[None]


def solution(mesh):
    placed = (P("slab", "row", "col"), P("slab", "row", "col"), P("slab", "row", "col"))
    return jax.shard_map(
        on_device, mesh=mesh, in_specs=placed, out_specs=P("slab", "row", "col"), check_vma=False
    )
```
